32 devices in a mesh: brick: 8 (over z, y), ch: 4 (over x, core).
Axes of the slice: x: 2, y: 2, z: 4, core: 2. Of those that a mesh axis runs over, the one named last changes fastest.
Arguments:
- features: bfloat16 [256, 1024], P('ch', 'brick'), may hold values from -6 to 6
- owner_map: int32 [1024, 1], P('brick'), may hold values from 0 to 7; in each aligned block of 128 rows (0 to 127, 128 to 255, ...) at most 32 rows name the same one
- kernel_map: int32 [27, 2048], P(None, 'brick'), may hold values from 0 to 320, as said below
- send_lists: int32 [2, 256], P(None, 'brick'), may hold values from 0 to 255
- drop_first: int32 [256, 2048], P('ch', 'brick'), may hold values 0 or 1
- drop_second: int32 [256, 2048], P('ch', 'brick'), may hold values 0 or 1
- weight_first: bfloat16 [27, 256, 256], P(None, 'ch'), may hold values from -0.15625 to 0.15625
- weight_second: bfloat16 [27, 256, 256], P(None, 'ch'), may hold values from -0.15625 to 0.15625
- cotangent: bfloat16 [256, 2048], P('ch', 'brick'), may hold values from -6 to 6
Outputs:
- block_out: bfloat16 [256, 2048], P('ch', 'brick')
- grad_features: bfloat16 [256, 1024], P('ch', 'brick')
- grad_weight_first: bfloat16 [27, 256, 256], P(None, 'ch')
- grad_weight_second: bfloat16 [27, 256, 256], P(None, 'ch')
The draws below stay inside these ranges and needn't reach their ends.
Inputs may be any that keep to these rules, and one draw needn't show every extreme that they name: `owner_map`: among the rows of one scan group, at most 32 are owned by the same brick. `kernel_map`: column 320 means that the neighbour is absent; in the middle offset row, slot i of every brick names column 32 + i.
All inputs are finite; a program needn't handle non-finite values. No bound on the sum of `drop_first` or of `drop_second` on one device may be relied on, other than what follows from the above.
Results may differ from the reference program's by a relative error of at most 0.0064.
Values may be sent and summed in bfloat16 or wider, within the bound.
No kernel may reach another device: no remote copies, remote signals or barrier semaphores. Data moves between devices by JAX's collectives and lax.ppermute only.
A program may use at most 64 MiB of HBM per device.

```python
import math
import jax
import jax.numpy as jnp
import numpy as np
from jax import lax

C = 256
KOFF = 27
SCAN_DEV = 128
BRICKS = 8
CAP = 32
SLOTS = 256
HALO = 32
EXT = 320
TOTAL_SLOTS = 2048


def draw_kernel_map(key, part):
    kind_key, inner_key, rim_key, side_key = jax.random.split(key, 4)
    shape = (KOFF, TOTAL_SLOTS)
    kinds = jax.random.randint(kind_key, shape, 0, 20)
    inner = jax.random.randint(inner_key, shape, HALO, HALO + SLOTS)
    border = jax.random.randint(rim_key, shape, 0, HALO)
    sides = jax.random.randint(side_key, shape, 0, 2)
    border = border + sides * (HALO + SLOTS)
    absent = SLOTS + 2 * HALO
    picked = jnp.where(kinds < 6, absent, jnp.where(kinds < 11, inner, border))
    centre = HALO + jnp.arange(TOTAL_SLOTS, dtype=jnp.int32) % SLOTS
    offsets = jnp.arange(KOFF, dtype=jnp.int32)[:, None]
    picked = jnp.where(offsets == KOFF // 2, centre[None, :], picked)
    picked = picked.at[0, 0].set(0)
    picked = picked.at[KOFF - 1, TOTAL_SLOTS - 1].set(absent)
    return picked.astype(jnp.int32)


def set_ends(result, stream_key, smallest, top_value):
    index_at = [jax.random.randint(jax.random.fold_in(stream_key, axis), (), 0, length) for axis, length in enumerate(result.shape)]
    main_axis = result.shape.index(max(result.shape))
    neighbour = index_at[:main_axis] + [(index_at[main_axis] + 1) % result.shape[main_axis]] + index_at[main_axis + 1:]
    return result.at[tuple(index_at)].set(smallest).at[tuple(neighbour)].set(top_value)


def with_spikes(array, stream_key, source, target, blocks, factor):
    owner, partner = [(jnp.arange(array.shape[position]) // (array.shape[position] // blocks)).reshape([-1 if axis == position else 1 for axis in range(array.ndim)]) for position in (source, target)]
    chosen = jax.random.permutation(stream_key, blocks)[partner]
    strong = (owner == chosen) | (owner == (partner + blocks // 2) % blocks)
    return jnp.where(strong, factor * array, array)


def block_levels(key, extent, pieces, low, largest):
    level, own = 1.0, jax.random.fold_in(key, 6)
    for position, blocks in pieces:
        steps = jnp.exp(jax.random.uniform(jax.random.fold_in(own, position), (blocks,), jnp.float32, low / len(pieces), largest / len(pieces)))
        level = level * jnp.repeat(steps, extent[position] // blocks).reshape([-1 if axis == position else 1 for axis in range(len(extent))])
    return level


def deal_out(key, own, number, rows, number_of, top, bound, lean):
    order = jax.random.permutation(key, number_of)
    heavy_load, common = load_shares(number_of, rows * top, bound, lean, True), load_shares(number_of, rows * top, bound, lean, False)
    places = jnp.arange(number_of)

    def named(lengths, turn):
        used = int((lengths > 0).sum())
        fixed = max(1, used // 4)
        shifted = fixed + (places - fixed + turn * (used - fixed)) % max(1, number_of - fixed)
        return jnp.zeros((number_of,), jnp.int32).at[order[jnp.where(places < fixed, places, shifted)]].set(jnp.asarray(lengths, jnp.int32))

    lengths = jnp.where(number % 4 == 0, named(heavy_load, number // 4), named(common, number - number // 4 - 1))
    mixed = jax.random.permutation(jax.random.fold_in(own, 3), number_of)
    donor, sink = mixed[0:number_of // 2 * 2:2], mixed[1:number_of // 2 * 2:2]
    room = jnp.minimum(lengths[donor] - 1, bound - lengths[sink]) // 2
    room = jnp.where((donor == order[0]) | (sink == order[0]) | (lengths[sink] == 0), 0, jnp.maximum(room, 0))
    shifted = jax.random.randint(jax.random.fold_in(own, 4), (number_of // 2,), 0, 1 << 20) % (room + 1)
    lengths = lengths.at[donor].add(-shifted).at[sink].add(shifted)
    items = jnp.searchsorted(jnp.cumsum(lengths), jnp.arange(rows * top), side="right").astype(jnp.int32)
    listing = items.reshape(top, rows).T
    listing = listing[jax.random.permutation(jax.random.fold_in(own, 1), rows)]
    turn = jax.random.randint(jax.random.fold_in(own, 2), (rows, 1), 0, top)
    return jnp.take_along_axis(listing, (jnp.arange(top)[None, :] + turn) % top, axis=1)


def load_shares(amount, total, limit, lean, full):
    weights = [(1 << 20) // math.isqrt(standing ** lean) + 1 for standing in range(1, amount + 1)]
    largest = limit if full else min(limit, max(-(-total // amount), total * weights[0] // sum(weights)))
    least = 1 if total - largest >= amount - 1 else 0
    holding, surplus = [largest] + [least] * (amount - 1), total - largest - least * (amount - 1)
    while surplus > 0:
        candidates = [i for i in range(1, amount) if holding[i] < largest] or [i for i in range(1, amount) if holding[i] < limit]
        mass, remaining = sum([weights[i] for i in candidates]), surplus
        for i in candidates:
            extra = min(limit - holding[i], max(1, remaining * weights[i] // mass), surplus)
            holding[i] = holding[i] + extra
            surplus = surplus - extra
    return np.array(holding)


def normal_values(own_key, dims, deviation, reach, shards=(), held_as=jnp.bfloat16):
    result = jax.random.normal(own_key, dims, jnp.float32) * deviation
    if len(shards) > 0:
        result = block_levels(own_key, dims, shards, -0.22, 0.18) * result
    return jnp.clip(result, min=-reach, max=reach).astype(held_as)


def gaussian_with(own_key, shape, spread, reach, shards, heavy, kind=jnp.bfloat16):
    result = spread * jax.random.normal(own_key, shape, jnp.float32)
    if shards:
        result = result * block_levels(own_key, shape, shards, -0.22, 0.18)
    return jnp.clip(with_spikes(result, jax.random.fold_in(own_key, 3), *heavy), -reach, reach).astype(kind)


def setup_inputs(seed: int = 0) -> dict:
    key_of = jax.random.split(jax.random.key(seed), 10)
    features = normal_values(key_of[0], (C, BRICKS * SCAN_DEV), 1.0, 6.0, ((0, 4), (1, 8)))
    owner_map_keys = jax.random.split(jax.random.fold_in(key_of[1], 1), (BRICKS * SCAN_DEV) // SCAN_DEV)
    owner_map_turns = jax.random.permutation(jax.random.fold_in(key_of[1], 3), (BRICKS * SCAN_DEV) // SCAN_DEV)
    owner_map = jax.vmap(lambda own, number: deal_out(jax.random.fold_in(key_of[1], 2), own, number, SCAN_DEV, BRICKS, 1, CAP, 1))(owner_map_keys, owner_map_turns).reshape((BRICKS * SCAN_DEV, 1))
    kernel_map = draw_kernel_map(jax.random.fold_in(key_of[9], 71), 0)
    send_lists = set_ends(jax.random.randint(key_of[3], (2, BRICKS * HALO), 0, SLOTS), jax.random.fold_in(key_of[3], 1), 0, SLOTS - 1).astype(jnp.int32)
    drop_first = set_ends((jax.random.randint(key_of[4], (C, TOTAL_SLOTS), 0, 10) < 9).astype(jnp.int32), jax.random.fold_in(key_of[4], 1), 0, 1)
    drop_second = set_ends((jax.random.randint(key_of[5], (C, TOTAL_SLOTS), 0, 10) < 9).astype(jnp.int32), jax.random.fold_in(key_of[5], 1), 0, 1)
    weight_first = normal_values(key_of[6], (KOFF, C, C), (KOFF * C // 4) ** -0.5, 0.15625, ((1, 4),))
    weight_second = normal_values(key_of[7], (KOFF, C, C), (KOFF * C // 4) ** -0.5, 0.15625, ((1, 4),))
    cotangent = gaussian_with(key_of[8], (C, TOTAL_SLOTS), 1.0, 6.0, ((0, 4), (1, 8)), (1, 0, 8, 2.0))
    return dict(features=features, owner_map=owner_map, kernel_map=kernel_map, send_lists=send_lists, drop_first=drop_first, drop_second=drop_second, weight_first=weight_first, weight_second=weight_second, cotangent=cotangent)


KEEP_RATE = 0.9


def slope_silu(value):
    sig = jax.nn.sigmoid(value)
    return sig * (1.0 + value * (1.0 - sig))


def relay_slots(owner_map):
    targets = owner_map[:, 0].reshape(BRICKS, SCAN_DEV).astype(jnp.int32)
    matches = (targets[:, :, None] == jnp.arange(BRICKS, dtype=jnp.int32)[None, None, :]).astype(jnp.int32)
    running = jnp.cumsum(matches, axis=1).astype(jnp.int32)
    ordinal = jnp.sum((running - 1) * matches, axis=2).astype(jnp.int32)
    source = jnp.arange(BRICKS, dtype=jnp.int32)[:, None]
    columns = (targets * SLOTS + source * CAP + ordinal).reshape(BRICKS * SCAN_DEV).astype(jnp.int32)
    tallies = jnp.sum(matches, axis=1).astype(jnp.int32)
    occupied = jnp.arange(CAP, dtype=jnp.int32)[None, None, :] < tallies.T[:, :, None]
    return columns, occupied.reshape(TOTAL_SLOTS).astype(jnp.float32)


def select_columns(block, indices):
    return jnp.take(block, indices, axis=1)


def add_columns(block, indices, values):
    return block.at[:, indices].add(values)


def extend(field, send_lists):
    blocks = field.reshape(C, BRICKS, SLOTS).transpose(1, 0, 2)
    to_previous_list = send_lists[0].reshape(BRICKS, HALO)
    to_next_list = send_lists[1].reshape(BRICKS, HALO)
    to_previous = jax.vmap(select_columns)(blocks, to_previous_list)
    to_next = jax.vmap(select_columns)(blocks, to_next_list)
    zero_rim = jnp.zeros((1, C, HALO), field.dtype)
    from_previous = jnp.concatenate([zero_rim, to_next[:-1]], axis=0)
    from_next = jnp.concatenate([to_previous[1:], zero_rim], axis=0)
    return jnp.concatenate([from_previous, blocks, from_next], axis=2)


def convolve(extended, offset_maps, weight):
    weight_full = weight.astype(jnp.float32)

    def single(element):
        brick_ext, brick_map = element
        gathered = jnp.take(brick_ext, brick_map, axis=1, mode="fill", fill_value=0).astype(jnp.float32)
        return jnp.einsum("ckr,kco->or", gathered, weight_full)

    results = lax.map(single, (extended, offset_maps))
    return results.transpose(1, 0, 2).reshape(C, TOTAL_SLOTS)


def transpose_conv(extended, offset_maps, grad, weight):
    grads = grad.reshape(C, BRICKS, SLOTS).transpose(1, 0, 2)
    weight_full = weight.astype(jnp.float32)

    def accumulate(summed_grad, element):
        brick_ext, brick_map, brick_grad = element
        gathered = jnp.take(brick_ext, brick_map, axis=1, mode="fill", fill_value=0).astype(jnp.float32)
        grad_full = brick_grad.astype(jnp.float32)
        summed_grad = summed_grad + jnp.einsum("ckr,or->kco", gathered, grad_full)
        pushed = jnp.einsum("kco,or->ckr", weight_full, grad_full)
        returned = jnp.zeros((C, EXT), jnp.float32).at[:, brick_map].add(pushed, mode="drop")
        return summed_grad, returned

    summed_grad, returned = lax.scan(accumulate, jnp.zeros((KOFF, C, C), jnp.float32), (extended, offset_maps, grads))
    return summed_grad, returned


def fold_back(returned, send_lists):
    to_previous_list = send_lists[0].reshape(BRICKS, HALO)
    to_next_list = send_lists[1].reshape(BRICKS, HALO)
    interior = returned[:, :, HALO:HALO + SLOTS]
    previous_part = returned[:, :, :HALO]
    next_part = returned[:, :, HALO + SLOTS:]
    zero_rim = jnp.zeros((1, C, HALO), jnp.float32)
    from_previous = jnp.concatenate([zero_rim, next_part[:-1]], axis=0)
    from_next = jnp.concatenate([previous_part[1:], zero_rim], axis=0)
    interior = jax.vmap(add_columns)(interior, to_previous_list, from_previous)
    interior = jax.vmap(add_columns)(interior, to_next_list, from_next)
    return interior.transpose(1, 0, 2).reshape(C, TOTAL_SLOTS)


def reference(features, owner_map, kernel_map, send_lists, drop_first, drop_second, weight_first, weight_second, cotangent):
    columns, occupied = relay_slots(owner_map)
    voxels = jnp.zeros((C, TOTAL_SLOTS), jnp.bfloat16).at[:, columns].set(features)
    keep_first = occupied[None, :] * drop_first.astype(jnp.float32) / KEEP_RATE
    keep_second = occupied[None, :] * drop_second.astype(jnp.float32) / KEEP_RATE
    offset_maps = kernel_map.reshape(KOFF, BRICKS, SLOTS).transpose(1, 0, 2)
    extended_voxels = extend(voxels, send_lists)
    conv_first = convolve(extended_voxels, offset_maps, weight_first)
    hidden = (jax.nn.silu(conv_first) * keep_first).astype(jnp.bfloat16)
    extended_hidden = extend(hidden, send_lists)
    conv_second = convolve(extended_hidden, offset_maps, weight_second)
    summed = voxels.astype(jnp.float32) + keep_second * conv_second
    block_out = jax.nn.silu(summed).astype(jnp.bfloat16)
    grad_pre = cotangent.astype(jnp.float32) * slope_silu(summed)
    grad_second = (grad_pre * keep_second).astype(jnp.bfloat16)
    weight_grad_second, returned_second = transpose_conv(extended_hidden, offset_maps, grad_second, weight_second)
    grad_hidden = fold_back(returned_second, send_lists)
    grad_first = (grad_hidden * keep_first * slope_silu(conv_first)).astype(jnp.bfloat16)
    weight_grad_first, returned_first = transpose_conv(extended_voxels, offset_maps, grad_first, weight_first)
    grad_voxels = (grad_pre + fold_back(returned_first, send_lists)).astype(jnp.bfloat16)
    grad_features = jnp.take(grad_voxels, columns, axis=1)
    factor = TOTAL_SLOTS ** -0.5
    return (block_out, grad_features, (weight_grad_first * factor).astype(jnp.bfloat16), (weight_grad_second * factor).astype(jnp.bfloat16))
```

```python
import functools

import jax
import jax.numpy as jnp
from jax import lax
from jax.experimental import pallas as pl
from jax.experimental.pallas import tpu as pltpu
from jax.sharding import PartitionSpec as P

KEEP_RATE = 0.9
BF = jnp.bfloat16
F32 = jnp.float32
INTERPRET = False


def slope_silu(value):
    sig = jax.nn.sigmoid(value)
    return sig * (1.0 + value * (1.0 - sig))


def nn(a, b):
    return lax.dot_general(a, b, (((1,), (0,)), ((), ())), preferred_element_type=F32)


def nt(a, b):
    return lax.dot_general(a, b, (((1,), (1,)), ((), ())), preferred_element_type=F32)


def hot(index_row, rows):
    shape = (rows, index_row.shape[1])
    row = lax.broadcasted_iota(jnp.int32, shape, 0)
    return jnp.where(row == index_row, 1.0, 0.0).astype(BF)


def loop(count, step, carry, group=3):
    group = group if count % group == 0 else 1

    def body(i, carry):
        for j in range(group):
            carry = step(i * group + j, carry)
        return carry

    return lax.fori_loop(0, count // group, body, carry)


def call(kernel, outs, scratch, args, ids, flops=10**9, vmem=40, name=None):
    single = not isinstance(outs, (list, tuple))
    outs = [outs] if single else list(outs)
    moved = sum(a.size * a.dtype.itemsize for a in args)
    moved += sum(o.size * jnp.dtype(o.dtype).itemsize for o in outs)
    result = pl.pallas_call(
        kernel,
        out_shape=outs,
        in_specs=[pl.BlockSpec(memory_space=pltpu.SMEM)]
        + [pl.BlockSpec(memory_space=pltpu.VMEM)] * len(args),
        out_specs=[pl.BlockSpec(memory_space=pltpu.VMEM)] * len(outs),
        scratch_shapes=scratch,
        compiler_params=None
        if INTERPRET
        else pltpu.CompilerParams(vmem_limit_bytes=vmem * 2**20),
        cost_estimate=pl.CostEstimate(flops=flops, bytes_accessed=moved, transcendentals=0),
        interpret=INTERPRET,
        name=name,
    )(ids, *args)
    return result[0] if single else result


class Sizes:
    def __init__(self, features, kernel_map, send_lists, nb, nc):
        self.nb, self.nc = nb, nc
        self.ch, self.scan = features.shape
        self.koff, self.slots = kernel_map.shape
        self.rim = send_lists.shape[1]
        self.cap = self.slots // nb
        self.hs = 4 * self.rim
        self.half = self.ch // 2
        self.kr = -(-(self.koff + 1) // 16) * 16
        self.rows = 2 * self.half + self.kr
        self.ext = self.slots + 2 * self.rim
        self.shift = self.ext // 2
        self.all = self.ch * nc
        self.depth = self.koff * self.ch


def pack_kernel(z, ids, feat, table, drop, out):
    h, lanes = z.half, z.scan
    out[0:h, 0:lanes] = feat[0:h, :]
    out[0:h, lanes : 2 * lanes] = feat[h : 2 * h, :]
    lend = hot(table[z.koff : z.koff + 1, lanes : lanes + z.hs], z.slots)
    chosen = nn(drop[...].astype(F32).astype(BF), lend).astype(BF)
    out[h : 2 * h, 0 : z.hs] = chosen[0:h, :]
    out[h : 2 * h, z.hs : 2 * z.hs] = chosen[h : 2 * h, :]
    row = lax.broadcasted_iota(jnp.int32, (z.kr, z.slots), 0)
    value = table[...] - jnp.where(row < z.koff, z.shift, 0)
    out[2 * h :, :] = value.astype(F32).astype(BF)


def read_table(z, pay, brick):
    return pay[brick, 2 * z.half :, :].astype(F32)


def lanes_of(shape):
    return lax.broadcasted_iota(jnp.int32, shape, len(shape) - 1)


def meta_row(z, pay, brick):
    return read_table(z, pay, brick)[z.koff : z.koff + 1, :].astype(jnp.int32)


def map_values(z, pay, brick):
    return read_table(z, pay, brick).astype(jnp.int32) + z.shift


def own_index(z, value):
    return value - z.rim


def halo_index(z, value):
    high = jnp.where(value >= z.rim + z.slots, value - z.slots + z.rim, -1)
    return jnp.where(value < z.rim, value + z.rim, high)


def gather_own(z, dst, table, halo, kmo, kmh):
    def step(k, carry):
        oh = hot(kmo[pl.ds(k, 1), :], z.slots)
        hh = hot(kmh[pl.ds(k, 1), :], z.hs)
        got = nn(table, oh) + nn(halo, hh)
        dst[pl.ds(pl.multiple_of(k * z.ch, z.ch), z.ch), 0 : z.slots] = got.astype(BF)
        return carry

    loop(z.koff, step, 0)


def halo_of(z, lent, a):
    lane = lanes_of(lent.shape[1:])
    none = jnp.zeros(lent.shape[1:], F32)
    low = lent[a - 1].astype(F32) if a > 0 else none
    high = lent[a + 1].astype(F32) if a < z.nb - 1 else none
    return jnp.where(lane < 2 * z.rim, low, high).astype(BF)


def first_kernel(z, ids, near, far, drop, wt, *rest):
    outs, (own, lent, stack, kmo, kmh, klo, klh) = rest[:-7], rest[-7:]
    parts, (keep, pay, vox, halo) = outs[: z.nc], outs[z.nc :]
    b, c = ids[0], ids[1]
    for q in range(z.nb):
        pay[b ^ q] = (near if q % 2 == 0 else far)[q // 2]
    for s in range(z.nb):
        own[s : s + 1, :] = read_table(z, pay, s)[z.koff : z.koff + 1, 0 : z.scan]
    columns = jnp.transpose(own[...])
    lane = lanes_of((z.scan, z.scan))
    sub = lax.broadcasted_iota(jnp.int32, (z.scan, z.scan), 0)
    key_lane = lanes_of((z.scan, z.slots)).astype(F32)
    ones = jnp.ones((16, z.scan), BF)
    for s in range(z.nb):
        mine = columns[:, s : s + 1]
        earlier = (mine == own[s : s + 1, :]) & (lane < sub)
        ordinal = jnp.sum(jnp.where(earlier, 1.0, 0.0), axis=1, keepdims=True)
        key = mine * z.cap + ordinal
        placed = jnp.where(key == key_lane, 1.0, 0.0).astype(BF)
        h = z.half
        rows = jnp.concatenate(
            [pay[s, 0:h, 0 : z.scan], pay[s, 0:h, z.scan : 2 * z.scan], ones], axis=0
        )
        moved = nn(rows, placed).astype(BF)
        for a in range(z.nb):
            vox[a, :, s * z.cap : (s + 1) * z.cap] = moved[:, a * z.cap : (a + 1) * z.cap]
    for a in range(z.nb):
        lend = hot(meta_row(z, pay, a)[:, z.scan : z.scan + z.hs], z.slots)
        lent[a] = nn(vox[a], lend).astype(BF)
    for a in range(z.nb):
        halo[a] = halo_of(z, lent, a)
    before, after = jnp.maximum(b - 1, 0), jnp.minimum(b + 1, z.nb - 1)
    value = map_values(z, pay, b)
    kmo[...] = own_index(z, value)
    kmh[...] = halo_index(z, value)
    hl = lanes_of((z.kr, z.hs))
    from_before = nn(
        pay[before, 2 * z.half :, :],
        hot(meta_row(z, pay, before)[:, z.scan : z.scan + z.hs], z.slots),
    )
    from_after = nn(
        pay[after, 2 * z.half :, :],
        hot(meta_row(z, pay, after)[:, z.scan : z.scan + z.hs], z.slots),
    )
    later = hl >= 2 * z.rim
    value = jnp.where(later, from_after, from_before).astype(jnp.int32) + z.shift
    index = own_index(z, value)
    inside = (index >= 0) & (index < z.slots)
    klo[...] = jnp.where(inside, index + jnp.where(later, z.slots, 0), -1)
    index = halo_index(z, value)
    klh[...] = jnp.where(index >= 0, index + jnp.where(later, z.hs, 0), -1)
    gather_own(z, stack, vox[b, 0 : z.ch, :], halo[b, 0 : z.ch, :], kmo, kmh)
    pair = jnp.concatenate([vox[before, 0 : z.ch, :], vox[after, 0 : z.ch, :]], axis=1)
    pair_halo = jnp.concatenate([halo[before, 0 : z.ch, :], halo[after, 0 : z.ch, :]], axis=1)

    def step(k, carry):
        oh = hot(klo[pl.ds(k, 1), :], 2 * z.slots)
        hh = hot(klh[pl.ds(k, 1), :], 2 * z.hs)
        got = nn(pair, oh) + nn(pair_halo, hh)
        rows = pl.ds(pl.multiple_of(k * z.ch, z.ch), z.ch)
        stack[rows, z.slots : z.slots + z.hs] = got.astype(BF)
        return carry

    loop(z.koff, step, 0)
    h = z.half
    kept = drop[...].astype(F32) * vox[b, z.ch : z.ch + 1, :].astype(F32)
    keep[:, 0 : z.slots] = kept / KEEP_RATE
    pick_before = jnp.concatenate([pay[before, h : 2 * h, 0 : z.hs], pay[before, h : 2 * h, z.hs : 2 * z.hs]], axis=0)
    pick_after = jnp.concatenate([pay[after, h : 2 * h, 0 : z.hs], pay[after, h : 2 * h, z.hs : 2 * z.hs]], axis=0)
    lane = lanes_of((z.ch, z.hs))
    picked = jnp.where(lane < 2 * z.rim, pick_before.astype(F32), pick_after.astype(F32))
    keep[:, z.slots :] = picked * halo[b, z.ch : z.ch + 1, :].astype(F32) / KEEP_RATE
    for j in range(z.nc):
        rows = pl.ds(pl.multiple_of((c ^ j) * z.ch, z.ch), z.ch)
        parts[j][...] = nn(wt[rows, :], stack[...]).astype(parts[j].dtype)


def second_kernel(z, ids, *rest):
    arrived, (keep, kmap, wt) = rest[: z.nc], rest[z.nc : z.nc + 3]
    outs, (stack, kmo, kmh) = rest[z.nc + 3 : -3], rest[-3:]
    parts, (conv, hidden) = outs[: z.nc], outs[z.nc :]
    c = ids[1]
    total = arrived[0][...]
    for part in arrived[1:]:
        total = total + part[...].astype(F32)
    made = (total * jax.nn.sigmoid(total) * keep[...]).astype(BF)
    conv[...] = total[:, 0 : z.slots]
    hidden[...] = made[:, 0 : z.slots]
    kmo[...] = own_index(z, kmap[...])
    kmh[...] = halo_index(z, kmap[...])
    gather_own(z, stack, made[:, 0 : z.slots], made[:, z.slots :], kmo, kmh)
    for j in range(z.nc):
        rows = pl.ds(pl.multiple_of((c ^ j) * z.ch, z.ch), z.ch)
        parts[j][...] = nn(wt[rows, :], stack[...]).astype(parts[j].dtype)


def third_kernel(z, ids, *rest):
    arrived, (vox, drop, cot) = rest[: z.nc], rest[z.nc : z.nc + 3]
    block, sends = rest[z.nc + 3], rest[z.nc + 4 :]
    b = ids[0]
    total = arrived[0][...]
    for part in arrived[1:]:
        total = total + part[...].astype(F32)
    keep = drop[...].astype(F32) * vox[b, z.ch : z.ch + 1, :].astype(F32) / KEEP_RATE
    summed = vox[b, 0 : z.ch, :].astype(F32) + keep * total
    block[...] = (summed * jax.nn.sigmoid(summed)).astype(BF)
    pre = cot[...].astype(F32) * slope_silu(summed)
    grad = (pre * keep).astype(BF)
    pre = pre.astype(BF)
    lane = lanes_of((1, 2 * z.cap))
    for i, send in enumerate(sends):
        first, other = b ^ (2 * i), b ^ (2 * i + 1)
        index = jnp.where(lane < z.cap, first * z.cap + lane, (other - 1) * z.cap + lane)
        send[:, 0 : z.slots] = grad
        send[:, z.slots :] = nn(pre, hot(index, z.slots)).astype(BF)


def collect(z, dst, ids, near, far):
    b, c = ids[0], ids[1]
    nz = z.nb // 2
    for i in range(z.nc // 2):
        for y in range(2):
            for k in range(nz):
                at = (i * 2 + y) * nz + k
                for low, source in ((0, near), (1, far)):
                    rows = pl.ds(pl.multiple_of((c ^ (2 * i + low)) * z.ch, z.ch), z.ch)
                    dst[b ^ (2 * k + y), rows, :] = source[at, :, 0 : z.slots]


def push(z, dst, weight, grad):
    count = z.koff
    size = z.depth // count

    def step(i, carry):
        rows = pl.ds(pl.multiple_of(i * size, size), size)
        dst[rows, :] = nn(weight[rows, :], grad).astype(BF)
        return carry

    loop(count, step, 0)


def fourth_kernel(z, ids, near, far, weight, pay, conv, keep, grad, gall, scan, pushed, kmo, kma, kmb):
    b = ids[0]
    collect(z, gall, ids, near, far)
    nz = z.nb // 2
    for q in range(z.nb):
        start = z.slots + (q % 2) * z.cap
        scan[b ^ q] = near[(q % 2) * nz + q // 2, :, start : start + z.cap]
    before, after = jnp.maximum(b - 1, 0), jnp.minimum(b + 1, z.nb - 1)
    push(z, pushed.at[0], weight, gall[b])
    push(z, pushed.at[1], weight, gall[before])
    push(z, pushed.at[2], weight, gall[after])
    kmo[...] = own_index(z, map_values(z, pay, b))
    value = map_values(z, pay, before)
    inside = (value >= z.rim + z.slots) & (value < z.ext) & (b > 0)
    kmb[...] = jnp.where(inside, value - z.slots + z.rim, -1)
    value = map_values(z, pay, after)
    kma[...] = jnp.where((value < z.rim) & (b < z.nb - 1), value + z.rim, -1)

    def step(k, carry):
        total, border = carry
        rows = pl.ds(pl.multiple_of(k * z.ch, z.ch), z.ch)
        one = pl.ds(k, 1)
        total = total + nt(pushed[0, rows, :], hot(kmo[one, :], z.slots))
        border = border + nt(pushed[1, rows, :], hot(kmb[one, :], z.hs))
        border = border + nt(pushed[2, rows, :], hot(kma[one, :], z.hs))
        return total, border

    total, border = loop(
        z.koff, step, (jnp.zeros((z.ch, z.slots), F32), jnp.zeros((z.ch, z.hs), F32))
    )
    lend = hot(meta_row(z, pay, b)[:, z.scan : z.scan + z.hs], z.slots)
    high = border.astype(BF)
    total = total + nt(high, lend) + nt((border - high.astype(F32)).astype(BF), lend)
    grad[...] = (total * keep[:, 0 : z.slots] * slope_silu(conv[...])).astype(BF)


def weight_sum(z, out, total, stack, kmo, kmh, table_at, halo_at, pay, gall):
    factor = float(z.nb * z.slots) ** (-0.5)
    pieces = 9 if z.koff % 9 == 0 else z.koff
    size = z.depth // pieces

    def brick(a, carry):
        value = map_values(z, pay, a)
        kmo[...] = own_index(z, value)
        kmh[...] = halo_index(z, value)
        gather_own(z, stack, table_at(a), halo_at(a), kmo, kmh)
        grads = gall[a]

        def piece(i, carry):
            rows = pl.ds(pl.multiple_of(i * size, size), size)
            total[rows, :] = total[rows, :] + nt(stack[rows, :], grads)
            return carry

        return loop(pieces, piece, carry)

    total[...] = jnp.zeros_like(total)
    lax.fori_loop(0, z.nb, brick, 0)
    out[...] = (total[...] * factor).astype(BF)


def second_weight_kernel(z, ids, near, far, pay, gall, out, total, stack, kmo, kmh, table, lent, halo):
    b = ids[0]
    for q in range(z.nb):
        table[b ^ q] = (near if q % 2 == 0 else far)[q // 2]
    for a in range(z.nb):
        lend = hot(meta_row(z, pay, a)[:, z.scan : z.scan + z.hs], z.slots)
        lent[a] = nn(table[a], lend).astype(BF)
    for a in range(z.nb):
        halo[a] = halo_of(z, lent, a)
    weight_sum(z, out, total, stack, kmo, kmh, lambda a: table[a], lambda a: halo[a], pay, gall)


def last_kernel(z, ids, near, far, weight, pay, vox, halo, scan, owner, out, wout, gall, pushed, total, stack, kmo, kmh):
    b = ids[0]
    collect(z, gall, ids, near, far)
    mine = owner[...].astype(F32)
    row = read_table(z, pay, b)[z.koff : z.koff + 1, 0 : z.scan]
    square = (z.scan, z.scan)
    lane = lanes_of(square)
    sub = lax.broadcasted_iota(jnp.int32, square, 0)
    earlier = (mine == row) & (lane < sub)
    ordinal = jnp.sum(jnp.where(earlier, 1.0, 0.0), axis=1, keepdims=True)
    slot = ordinal + (b * z.cap).astype(F32)
    at = lax.broadcasted_iota(jnp.int32, (z.hs, z.slots), 0)
    wanted = jnp.where(at < z.rim, z.rim + b * z.cap + at, -5)
    if z.cap < z.rim:
        wanted = jnp.where(at < z.cap, wanted, -5)
    wanted = jnp.where((at >= z.rim) & (at < 2 * z.rim), at - z.rim, wanted)
    wanted = jnp.where((at >= 2 * z.rim) & (at < 3 * z.rim), at + z.slots - z.rim, wanted)
    target = lanes_of((1, z.hs))

    def brick(a, result):
        push(z, pushed, weight, gall[a])
        kmo[...] = map_values(z, pay, a)

        def step(k, got):
            rows = pl.ds(pl.multiple_of(k * z.ch, z.ch), z.ch)
            chosen = jnp.where(wanted == kmo[pl.ds(k, 1), :], 1.0, 0.0).astype(BF)
            return got + nt(pushed[rows, :], chosen)

        got = loop(z.koff, step, jnp.zeros((z.ch, z.hs), F32))
        before, after = jnp.maximum(a - 1, 0), jnp.minimum(a + 1, z.nb - 1)
        low = meta_row(z, pay, before)[:, z.scan : z.scan + z.hs]
        high = meta_row(z, pay, after)[:, z.scan : z.scan + z.hs]
        holder = jnp.where(target < z.rim, a, jnp.where(target < 2 * z.rim, a - 1, a + 1))
        where = jnp.where(target < z.rim, b * z.cap + target, jnp.where(target < 2 * z.rim, low, high))
        place = jnp.where((mine == holder.astype(F32)) & (slot == where.astype(F32)), 1.0, 0.0).astype(BF)
        big = got.astype(BF)
        result = result + nt(big, place) + nt((got - big.astype(F32)).astype(BF), place)
        target_own = lanes_of((1, z.cap))
        place = jnp.where((mine == jnp.asarray(a, F32)) & (ordinal == target_own.astype(F32)), 1.0, 0.0).astype(BF)
        return result + nt(scan[a], place)

    result = lax.fori_loop(0, z.nb, brick, jnp.zeros((z.ch, z.scan), F32))
    out[...] = result.astype(BF)
    weight_sum(z, wout, total, stack, kmo, kmh, lambda a: vox[a, 0 : z.ch, :], lambda a: halo[a, 0 : z.ch, :], pay, gall)


def swap(value, axis, mask):
    count = lax.axis_size(axis)
    return lax.ppermute(value, axis, [(i ^ mask, i) for i in range(count)])


def swap_both(value, brick_mask, ch_mask):
    if ch_mask == 0:
        return swap(value, "brick", brick_mask)
    if brick_mask == 0:
        return swap(value, "ch", ch_mask)
    nb, nc = lax.axis_size("brick"), lax.axis_size("ch")
    pairs = [
        ((b ^ brick_mask) * nc + (c ^ ch_mask), b * nc + c) for b in range(nb) for c in range(nc)
    ]
    return lax.ppermute(value, ("brick", "ch"), pairs)


def over_even(blocks, count):
    return jnp.stack(
        [blocks[0]] + [swap(blocks[i], "brick", 2 * i) for i in range(1, count // 2)]
    )


def over_bricks(block, nb):
    near = over_even([block] * (nb // 2), nb)
    return near, swap(near, "brick", 1)


def over_all(blocks, nb, nc):
    plane = over_even(blocks, nb)
    parts = [plane]
    for i in range(nc // 2):
        for y in range(2):
            if i or y:
                parts.append(swap_both(plane, y, 2 * i))
    near = jnp.concatenate(parts, axis=0)
    return near, swap(near, "ch", 1)


def gathered_local(
    features,
    owner_map,
    kernel_map,
    send_lists,
    drop_first,
    drop_second,
    weight_first,
    weight_second,
    cotangent,
):
    nb, nc = lax.axis_size("brick"), lax.axis_size("ch")
    z = Sizes(features, kernel_map, send_lists, nb, nc)
    ids = jnp.stack([lax.axis_index("brick"), lax.axis_index("ch")]).astype(jnp.int32)
    sds = jax.ShapeDtypeStruct
    vm = pltpu.VMEM
    pad = jnp.full((1, z.rim), -1, jnp.int32)
    meta = jnp.concatenate([owner_map.reshape(1, z.scan), pad, send_lists[1:2], send_lists[0:1], pad], axis=1)
    table = jnp.concatenate(
        [kernel_map, meta, jnp.zeros((z.kr - z.koff - 1, z.slots), jnp.int32)], axis=0
    )
    flat_first = weight_first.reshape(z.depth, z.all)
    flat_second = weight_second.reshape(z.depth, z.all)
    turned_first = flat_first.T
    turned_second = flat_second.T

    payload = call(
        functools.partial(pack_kernel, z),
        sds((z.rows, z.slots), BF),
        [],
        [features, table, drop_first],
        ids,
        name="pack",
    )
    near, far = over_bricks(payload, nb)
    wide = z.slots + z.hs
    ints = [vm((z.kr, z.slots), jnp.int32)] * 2
    *parts, keep, pay, vox, halo = call(
        functools.partial(first_kernel, z),
        [sds((z.ch, wide), F32)]
        + [sds((z.ch, wide), BF)] * (nc - 1)
        + [
            sds((z.ch, wide), F32),
            sds((nb, z.rows, z.slots), BF),
            sds((nb, z.ch + 16, z.slots), BF),
            sds((nb, z.ch + 16, z.hs), BF),
        ],
        [
            vm((nb, z.scan), F32),
            vm((nb, z.ch + 16, z.hs), BF),
            vm((z.depth, wide), BF),
            *ints,
            vm((z.kr, z.hs), jnp.int32),
            vm((z.kr, z.hs), jnp.int32),
        ],
        [near, far, drop_first, turned_first],
        ids,
        name="first",
    )
    arrived = [parts[0]] + [swap(parts[j], "ch", j) for j in range(1, nc)]
    small = [vm((z.koff, z.slots), jnp.int32)] * 2
    *parts, conv, hidden = call(
        functools.partial(second_kernel, z),
        [sds((z.ch, z.slots), F32)]
        + [sds((z.ch, z.slots), BF)] * (nc - 1)
        + [sds((z.ch, z.slots), F32), sds((z.ch, z.slots), BF)],
        [vm((z.depth, z.slots), BF), *small],
        [*arrived, keep, kernel_map, turned_second],
        ids,
        name="second",
    )
    arrived = [parts[0]] + [swap(parts[j], "ch", j) for j in range(1, nc)]
    block_out, *sends = call(
        functools.partial(third_kernel, z),
        [sds((z.ch, z.slots), BF)] + [sds((z.ch, z.slots + 2 * z.cap), BF)] * (nb // 2),
        [],
        [*arrived, vox, drop_second, cotangent],
        ids,
        name="third",
    )
    hidden_near, hidden_far = over_bricks(hidden, nb)
    near, far = over_all(sends, nb, nc)
    grad_first, gall, scan = call(
        functools.partial(fourth_kernel, z),
        [
            sds((z.ch, z.slots), BF),
            sds((nb, z.all, z.slots), BF),
            sds((nb, z.ch, z.cap), BF),
        ],
        [
            vm((3, z.depth, z.slots), BF),
            vm((z.kr, z.slots), jnp.int32),
            vm((z.kr, z.slots), jnp.int32),
            vm((z.kr, z.slots), jnp.int32),
        ],
        [near, far, flat_second, pay, conv, keep],
        ids,
        name="fourth",
    )
    weight_grad_second = call(
        functools.partial(second_weight_kernel, z),
        sds((z.depth, z.all), BF),
        [
            vm((z.depth, z.all), F32),
            vm((z.depth, z.slots), BF),
            *ints,
            vm((nb, z.ch, z.slots), BF),
            vm((nb, z.ch, z.hs), BF),
            vm((nb, z.ch, z.hs), BF),
        ],
        [hidden_near, hidden_far, pay, gall],
        ids,
        name="second_weight",
    )
    near, far = over_all([grad_first] * (nb // 2), nb, nc)
    grad_features, weight_grad_first = call(
        functools.partial(last_kernel, z),
        [sds((z.ch, z.scan), BF), sds((z.depth, z.all), BF)],
        [
            vm((nb, z.all, z.slots), BF),
            vm((z.depth, z.slots), BF),
            vm((z.depth, z.all), F32),
            vm((z.depth, z.slots), BF),
            *ints,
        ],
        [near, far, flat_first, pay, vox, halo, scan, owner_map],
        ids,
        name="last",
    )
    return (
        block_out,
        grad_features,
        weight_grad_first.reshape(weight_first.shape),
        weight_grad_second.reshape(weight_second.shape),
    )


def with_halo(block, sides, width):
    for axis, dim in sides:
        count = lax.axis_size(axis)
        forward = [(i, i + 1) for i in range(count - 1)]
        backward = [(target, source) for source, target in forward]
        low = lax.ppermute(
            lax.slice_in_dim(block, block.shape[dim] - width, None, axis=dim), axis, forward
        )
        high = lax.ppermute(lax.slice_in_dim(block, 0, width, axis=dim), axis, backward)
        block = jnp.concatenate([low, block, high], axis=dim)
    return block


def spread(field, send_lists):
    rim_width = send_lists.shape[1]
    outgoing = jnp.concatenate(
        [jnp.take(field, send_lists[0], axis=1), jnp.take(field, send_lists[1], axis=1)], axis=1
    )
    padded = with_halo(outgoing, (("brick", 1),), rim_width)
    return jnp.concatenate([padded[:, :rim_width], field, padded[:, 3 * rim_width :]], axis=1)


def convolve(extended, kernel_map, weight):
    gathered = jnp.take(extended, kernel_map, axis=1, mode="fill", fill_value=0)
    return (
        lax.psum_scatter(
            jnp.einsum("ckr,kco->or", gathered, weight, preferred_element_type=jnp.float32),
            "ch",
            scatter_dimension=0,
            tiled=True,
        ),
        gathered,
    )


def adjoint(gathered, kernel_map, grad_local, weight, extent):
    gathered_grad = lax.all_gather(grad_local, "ch", axis=0, tiled=True)
    weight_grad = jnp.einsum(
        "ckr,or->kco", gathered, gathered_grad, preferred_element_type=jnp.float32
    )
    pushed = jnp.einsum("kco,or->ckr", weight, gathered_grad, preferred_element_type=jnp.float32)
    returned = (
        jnp.zeros((pushed.shape[0], extent), jnp.float32).at[:, kernel_map].add(pushed, mode="drop")
    )
    return (weight_grad, returned)


def fold_back(returned, send_lists, slot_count):
    rim_width = send_lists.shape[1]
    borders = jnp.concatenate(
        [returned[:, :rim_width], returned[:, rim_width + slot_count :]], axis=1
    )
    padded = with_halo(borders, (("brick", 1),), rim_width)
    interior = returned[:, rim_width : rim_width + slot_count]
    interior = interior.at[:, send_lists[0]].add(padded[:, :rim_width])
    return interior.at[:, send_lists[1]].add(padded[:, 3 * rim_width :])


def summed_local(
    features,
    owner_map,
    kernel_map,
    send_lists,
    drop_first,
    drop_second,
    weight_first,
    weight_second,
    cotangent,
):
    bricks = lax.axis_size("brick")
    channels = features.shape[0]
    slot_count = 2 * features.shape[1]
    capacity = slot_count // bricks
    targets = owner_map[:, 0]
    matches = (targets[:, None] == jnp.arange(bricks, dtype=jnp.int32)[None, :]).astype(jnp.int32)
    running = jnp.cumsum(matches, axis=0)
    ordinal = jnp.sum((running - 1) * matches, axis=1)
    columns = targets * capacity + ordinal
    outgoing = jnp.zeros((channels, slot_count), features.dtype).at[:, columns].set(features)
    tallies = jnp.sum(matches, axis=0)[None, :].astype(jnp.bfloat16)
    arrived, arrived_tallies = (
        lax.all_to_all(
            outgoing.reshape(channels, bricks, capacity),
            "brick",
            split_axis=1,
            concat_axis=1,
            tiled=True,
        ),
        lax.all_to_all(tallies, "brick", split_axis=1, concat_axis=1, tiled=True),
    )
    voxels = arrived.reshape(channels, slot_count)
    occupied = (
        jnp.arange(capacity, dtype=jnp.int32)[None, :]
        < arrived_tallies[0].astype(jnp.int32)[:, None]
    )
    occupied = occupied.reshape(slot_count).astype(jnp.float32)
    keep_first = occupied[None, :] * drop_first.astype(jnp.float32) / KEEP_RATE
    keep_second = occupied[None, :] * drop_second.astype(jnp.float32) / KEEP_RATE
    extended_voxels = spread(voxels, send_lists)
    extent = extended_voxels.shape[1]
    conv_first, gathered_voxels = convolve(extended_voxels, kernel_map, weight_first)
    hidden = (jax.nn.silu(conv_first) * keep_first).astype(jnp.bfloat16)
    extended_hidden = spread(hidden, send_lists)
    conv_second, gathered_hidden = convolve(extended_hidden, kernel_map, weight_second)
    summed = voxels.astype(jnp.float32) + keep_second * conv_second
    block_out = jax.nn.silu(summed).astype(jnp.bfloat16)
    grad_pre = cotangent.astype(jnp.float32) * slope_silu(summed)
    grad_second = (grad_pre * keep_second).astype(jnp.bfloat16)
    weight_grad_second, returned_second = adjoint(
        gathered_hidden, kernel_map, grad_second, weight_second, extent
    )
    grad_hidden = fold_back(returned_second, send_lists, slot_count)
    grad_first = (grad_hidden * keep_first * slope_silu(conv_first)).astype(jnp.bfloat16)
    weight_grad_first, returned_first = adjoint(
        gathered_voxels, kernel_map, grad_first, weight_first, extent
    )
    weight_grad_first, weight_grad_second = lax.psum(
        (weight_grad_first, weight_grad_second), "brick"
    )
    grad_voxels = (grad_pre + fold_back(returned_first, send_lists, slot_count)).astype(
        jnp.bfloat16
    )
    homeward = lax.all_to_all(
        grad_voxels.reshape(channels, bricks, capacity),
        "brick",
        split_axis=1,
        concat_axis=1,
        tiled=True,
    )
    grad_features = jnp.take(homeward.reshape(channels, slot_count), columns, axis=1)
    factor = float(bricks * slot_count) ** (-0.5)
    return (
        block_out,
        grad_features,
        (weight_grad_first * factor).astype(jnp.bfloat16),
        (weight_grad_second * factor).astype(jnp.bfloat16),
    )


def local(features, owner_map, kernel_map, *rest):
    nb, nc = lax.axis_size("brick"), lax.axis_size("ch")
    channels = features.shape[0]
    gather = nb * kernel_map.shape[1] <= 2 * kernel_map.shape[0] * channels
    even = all(n > 1 and n & (n - 1) == 0 for n in (nb, nc))
    scan, slots, rim = features.shape[1], kernel_map.shape[1], rest[0].shape[1]
    fits = slots <= nb * rim and slots == 2 * scan and 4 * rim <= scan
    plan = gathered_local if gather and even and fits else summed_local
    return plan(features, owner_map, kernel_map, *rest)


def solution(mesh):
    return jax.shard_map(
        local,
        mesh=mesh,
        in_specs=(
            P("ch", "brick"),
            P("brick", None),
            P(None, "brick"),
            P(None, "brick"),
            P("ch", "brick"),
            P("ch", "brick"),
            P(None, "ch", None),
            P(None, "ch", None),
            P("ch", "brick"),
        ),
        out_specs=(P("ch", "brick"), P("ch", "brick"), P(None, "ch", None), P(None, "ch", None)),
        check_vma=False,
    )
```

```python
import functools

import jax
import jax.numpy as jnp
from jax import lax
from jax.experimental import pallas as pl
from jax.experimental.pallas import tpu as pltpu
from jax.sharding import PartitionSpec as P

KEEP_RATE = 0.9
BF = jnp.bfloat16
F32 = jnp.float32
INTERPRET = False


def slope_silu(value):
    sig = jax.nn.sigmoid(value)
    return sig * (1.0 + value * (1.0 - sig))


def nn(a, b):
    return lax.dot_general(a, b, (((1,), (0,)), ((), ())), preferred_element_type=F32)


def nt(a, b):
    return lax.dot_general(a, b, (((1,), (1,)), ((), ())), preferred_element_type=F32)


def hot(index_row, rows):
    shape = (rows, index_row.shape[1])
    row = lax.broadcasted_iota(jnp.int32, shape, 0)
    return jnp.where(row == index_row, 1.0, 0.0).astype(BF)


def loop(count, step, carry):
    for i in range(count):
        carry = step(i, carry)
    return carry


def call(kernel, outs, scratch, args, ids, flops=10**9, vmem=12, name=None):
    single = not isinstance(outs, (list, tuple))
    outs = [outs] if single else list(outs)
    moved = sum(a.size * a.dtype.itemsize for a in args)
    moved += sum(o.size * jnp.dtype(o.dtype).itemsize for o in outs)
    result = pl.pallas_call(
        kernel,
        out_shape=outs,
        in_specs=[pl.BlockSpec(memory_space=pltpu.SMEM)]
        + [pl.BlockSpec(memory_space=pltpu.VMEM)] * len(args),
        out_specs=[pl.BlockSpec(memory_space=pltpu.VMEM)] * len(outs),
        scratch_shapes=scratch,
        compiler_params=None
        if INTERPRET
        else pltpu.CompilerParams(vmem_limit_bytes=vmem * 2**20),
        cost_estimate=pl.CostEstimate(flops=flops, bytes_accessed=moved, transcendentals=0),
        interpret=INTERPRET,
        name=name,
    )(ids, *args)
    return result[0] if single else result


class Sizes:
    def __init__(self, features, kernel_map, send_lists, nb, nc):
        self.nb, self.nc = nb, nc
        self.ch, self.scan = features.shape
        self.koff, self.slots = kernel_map.shape
        self.rim = send_lists.shape[1]
        self.cap = self.slots // nb
        self.hs = 4 * self.rim
        self.half = self.ch // 2
        self.kr = -(-(self.koff + 1) // 16) * 16
        self.rows = 2 * self.half + self.kr
        self.ext = self.slots + 2 * self.rim
        self.shift = self.ext // 2
        self.all = self.ch * nc
        self.depth = self.koff * self.ch


def pack_kernel(z, ids, feat, owner, kmap, lists, drop, out, table):
    h, lanes = z.half, z.scan
    out[0:h, 0:lanes] = feat[0:h, :]
    out[0:h, lanes : 2 * lanes] = feat[h : 2 * h, :]
    table[...] = jnp.full(table.shape, -1, jnp.int32)
    table[0 : z.koff, :] = kmap[...] - z.shift
    meta = slice(z.koff, z.koff + 1)
    table[meta, 0:lanes] = owner[...]
    table[meta, lanes + z.rim : lanes + 2 * z.rim] = lists[1:2, :]
    table[meta, lanes + 2 * z.rim : lanes + 3 * z.rim] = lists[0:1, :]
    lend = hot(table[meta, lanes : lanes + z.hs], z.slots)
    chosen = nn(drop[...].astype(F32).astype(BF), lend).astype(BF)
    out[h : 2 * h, 0 : z.hs] = chosen[0:h, :]
    out[h : 2 * h, z.hs : 2 * z.hs] = chosen[h : 2 * h, :]
    out[2 * h :, :] = table[...].astype(F32).astype(BF)


def read_table(z, pay, brick):
    return pay[brick, 2 * z.half :, :].astype(F32)


def lanes_of(shape):
    return lax.broadcasted_iota(jnp.int32, shape, len(shape) - 1)


def meta_row(z, pay, brick):
    return read_table(z, pay, brick)[z.koff : z.koff + 1, :].astype(jnp.int32)


def map_values(z, pay, brick):
    return read_table(z, pay, brick).astype(jnp.int32) + z.shift


def own_index(z, value):
    return value - z.rim


def halo_index(z, value):
    high = jnp.where(value >= z.rim + z.slots, value - z.slots + z.rim, -1)
    return jnp.where(value < z.rim, value + z.rim, high)


def gather_own(z, dst, table, halo, kmo, kmh):
    def step(k, carry):
        oh = hot(kmo[pl.ds(k, 1), :], z.slots)
        hh = hot(kmh[pl.ds(k, 1), :], z.hs)
        got = nn(table, oh) + nn(halo, hh)
        dst[pl.ds(k * z.ch, z.ch), 0 : z.slots] = got.astype(BF)
        return carry

    loop(z.koff, step, 0)


def halo_of(z, lent, a):
    lane = lanes_of(lent.shape[1:])
    none = jnp.zeros(lent.shape[1:], F32)
    low = lent[a - 1].astype(F32) if a > 0 else none
    high = lent[a + 1].astype(F32) if a < z.nb - 1 else none
    return jnp.where(lane < 2 * z.rim, low, high).astype(BF)


def first_kernel(z, ids, near, far, drop, wt, *rest):
    outs, (own, lent, stack, kmo, kmh, klo, klh) = rest[:-7], rest[-7:]
    parts, (keep, pay, vox, halo) = outs[: z.nc], outs[z.nc :]
    b, c = ids[0], ids[1]
    for q in range(z.nb):
        pay[b ^ q] = (near if q % 2 == 0 else far)[q // 2]
    for s in range(z.nb):
        own[s : s + 1, :] = read_table(z, pay, s)[z.koff : z.koff + 1, 0 : z.scan]
    columns = jnp.transpose(own[...])
    lane = lanes_of((z.scan, z.scan))
    sub = lax.broadcasted_iota(jnp.int32, (z.scan, z.scan), 0)
    key_lane = lanes_of((z.scan, z.slots)).astype(F32)
    ones = jnp.ones((16, z.scan), BF)
    for s in range(z.nb):
        mine = columns[:, s : s + 1]
        earlier = (mine == own[s : s + 1, :]) & (lane < sub)
        ordinal = jnp.sum(jnp.where(earlier, 1.0, 0.0), axis=1, keepdims=True)
        key = mine * z.cap + ordinal
        placed = jnp.where(key == key_lane, 1.0, 0.0).astype(BF)
        h = z.half
        rows = jnp.concatenate(
            [pay[s, 0:h, 0 : z.scan], pay[s, 0:h, z.scan : 2 * z.scan], ones], axis=0
        )
        moved = nn(rows, placed).astype(BF)
        for a in range(z.nb):
            vox[a, :, s * z.cap : (s + 1) * z.cap] = moved[:, a * z.cap : (a + 1) * z.cap]
    for a in range(z.nb):
        lend = hot(meta_row(z, pay, a)[:, z.scan : z.scan + z.hs], z.slots)
        lent[a] = nn(vox[a], lend).astype(BF)
    for a in range(z.nb):
        halo[a] = halo_of(z, lent, a)
    before, after = jnp.maximum(b - 1, 0), jnp.minimum(b + 1, z.nb - 1)
    value = map_values(z, pay, b)
    kmo[...] = own_index(z, value)
    kmh[...] = halo_index(z, value)
    hl = lanes_of((z.kr, z.hs))
    from_before = nn(
        pay[before, 2 * z.half :, :],
        hot(meta_row(z, pay, before)[:, z.scan : z.scan + z.hs], z.slots),
    )
    from_after = nn(
        pay[after, 2 * z.half :, :],
        hot(meta_row(z, pay, after)[:, z.scan : z.scan + z.hs], z.slots),
    )
    later = hl >= 2 * z.rim
    value = jnp.where(later, from_after, from_before).astype(jnp.int32) + z.shift
    index = own_index(z, value)
    inside = (index >= 0) & (index < z.slots)
    klo[...] = jnp.where(inside, index + jnp.where(later, z.slots, 0), -1)
    index = halo_index(z, value)
    klh[...] = jnp.where(index >= 0, index + jnp.where(later, z.hs, 0), -1)
    gather_own(z, stack, vox[b, 0 : z.ch, :], halo[b, 0 : z.ch, :], kmo, kmh)
    pair = jnp.concatenate([vox[before, 0 : z.ch, :], vox[after, 0 : z.ch, :]], axis=1)
    pair_halo = jnp.concatenate([halo[before, 0 : z.ch, :], halo[after, 0 : z.ch, :]], axis=1)

    def step(k, carry):
        oh = hot(klo[pl.ds(k, 1), :], 2 * z.slots)
        hh = hot(klh[pl.ds(k, 1), :], 2 * z.hs)
        got = nn(pair, oh) + nn(pair_halo, hh)
        rows = pl.ds(k * z.ch, z.ch)
        stack[rows, z.slots : z.slots + z.hs] = got.astype(BF)
        return carry

    loop(z.koff, step, 0)
    h = z.half
    kept = drop[...].astype(F32) * vox[b, z.ch : z.ch + 1, :].astype(F32)
    keep[:, 0 : z.slots] = kept / KEEP_RATE
    pick_before = jnp.concatenate([pay[before, h : 2 * h, 0 : z.hs], pay[before, h : 2 * h, z.hs : 2 * z.hs]], axis=0)
    pick_after = jnp.concatenate([pay[after, h : 2 * h, 0 : z.hs], pay[after, h : 2 * h, z.hs : 2 * z.hs]], axis=0)
    lane = lanes_of((z.ch, z.hs))
    picked = jnp.where(lane < 2 * z.rim, pick_before.astype(F32), pick_after.astype(F32))
    keep[:, z.slots :] = picked * halo[b, z.ch : z.ch + 1, :].astype(F32) / KEEP_RATE
    for j in range(z.nc):
        rows = pl.ds(pl.multiple_of((c ^ j) * z.ch, z.ch), z.ch)
        parts[j][...] = nn(wt[rows, :], stack[...]).astype(parts[j].dtype)


def second_kernel(z, ids, *rest):
    arrived, (keep, kmap, wt) = rest[: z.nc], rest[z.nc : z.nc + 3]
    outs, (stack, kmo, kmh) = rest[z.nc + 3 : -3], rest[-3:]
    parts, (conv, hidden) = outs[: z.nc], outs[z.nc :]
    c = ids[1]
    total = arrived[0][...]
    for part in arrived[1:]:
        total = total + part[...].astype(F32)
    made = (total * jax.nn.sigmoid(total) * keep[...]).astype(BF)
    conv[...] = total[:, 0 : z.slots]
    hidden[...] = made[:, 0 : z.slots]
    kmo[...] = own_index(z, kmap[...])
    kmh[...] = halo_index(z, kmap[...])
    gather_own(z, stack, made[:, 0 : z.slots], made[:, z.slots :], kmo, kmh)
    for j in range(z.nc):
        rows = pl.ds(pl.multiple_of((c ^ j) * z.ch, z.ch), z.ch)
        parts[j][...] = nn(wt[rows, :], stack[...]).astype(parts[j].dtype)


def third_kernel(z, ids, *rest):
    arrived, (vox, drop, cot) = rest[: z.nc], rest[z.nc : z.nc + 3]
    block, sends = rest[z.nc + 3], rest[z.nc + 4 :]
    b = ids[0]
    total = arrived[0][...]
    for part in arrived[1:]:
        total = total + part[...].astype(F32)
    keep = drop[...].astype(F32) * vox[b, z.ch : z.ch + 1, :].astype(F32) / KEEP_RATE
    summed = vox[b, 0 : z.ch, :].astype(F32) + keep * total
    block[...] = (summed * jax.nn.sigmoid(summed)).astype(BF)
    pre = cot[...].astype(F32) * slope_silu(summed)
    grad = (pre * keep).astype(BF)
    pre = pre.astype(BF)
    lane = lanes_of((1, 2 * z.cap))
    for i, send in enumerate(sends):
        first, other = b ^ (2 * i), b ^ (2 * i + 1)
        index = jnp.where(lane < z.cap, first * z.cap + lane, (other - 1) * z.cap + lane)
        send[:, 0 : z.slots] = grad
        send[:, z.slots :] = nn(pre, hot(index, z.slots)).astype(BF)


def collect(z, dst, ids, near, far):
    b, c = ids[0], ids[1]
    nz = z.nb // 2
    for i in range(z.nc // 2):
        for y in range(2):
            for k in range(nz):
                at = (i * 2 + y) * nz + k
                for low, source in ((0, near), (1, far)):
                    rows = pl.ds(pl.multiple_of((c ^ (2 * i + low)) * z.ch, z.ch), z.ch)
                    dst[b ^ (2 * k + y), rows, :] = source[at, :, 0 : z.slots]


def push(z, dst, weight, grad):
    pieces = 3 if z.koff % 3 == 0 else z.koff
    size = z.depth // pieces
    for i in range(pieces):
        rows = slice(i * size, (i + 1) * size)
        dst[rows, :] = nn(weight[rows, :], grad).astype(BF)


def fourth_kernel(z, ids, near, far, weight, pay, conv, keep, grad, gall, scan, pushed, kmo, kma, kmb):
    b = ids[0]
    collect(z, gall, ids, near, far)
    nz = z.nb // 2
    for q in range(z.nb):
        start = z.slots + (q % 2) * z.cap
        scan[b ^ q] = near[(q % 2) * nz + q // 2, :, start : start + z.cap]
    before, after = jnp.maximum(b - 1, 0), jnp.minimum(b + 1, z.nb - 1)
    push(z, pushed.at[0], weight, gall[b])
    push(z, pushed.at[1], weight, gall[before])
    push(z, pushed.at[2], weight, gall[after])
    kmo[...] = own_index(z, map_values(z, pay, b))
    value = map_values(z, pay, before)
    inside = (value >= z.rim + z.slots) & (value < z.ext) & (b > 0)
    kmb[...] = jnp.where(inside, value - z.slots + z.rim, -1)
    value = map_values(z, pay, after)
    kma[...] = jnp.where((value < z.rim) & (b < z.nb - 1), value + z.rim, -1)

    def step(k, carry):
        total, border = carry
        rows = pl.ds(k * z.ch, z.ch)
        one = pl.ds(k, 1)
        total = total + nt(pushed[0, rows, :], hot(kmo[one, :], z.slots))
        border = border + nt(pushed[1, rows, :], hot(kmb[one, :], z.hs))
        border = border + nt(pushed[2, rows, :], hot(kma[one, :], z.hs))
        return total, border

    total, border = loop(
        z.koff, step, (jnp.zeros((z.ch, z.slots), F32), jnp.zeros((z.ch, z.hs), F32))
    )
    lend = hot(meta_row(z, pay, b)[:, z.scan : z.scan + z.hs], z.slots)
    high = border.astype(BF)
    total = total + nt(high, lend) + nt((border - high.astype(F32)).astype(BF), lend)
    grad[...] = (total * keep[:, 0 : z.slots] * slope_silu(conv[...])).astype(BF)


def gather_kernel(z, first, count, ids, pay, table, halo, out, kmo, kmh):
    def brick(i, carry):
        value = map_values(z, pay, first + i)
        kmo[...] = own_index(z, value)
        kmh[...] = halo_index(z, value)
        a = first + i
        gather_own(z, out.at[i], table[a, 0 : z.ch, :], halo[a, 0 : z.ch, :], kmo, kmh)
        return carry

    lax.fori_loop(0, count, brick, 0)


def table_kernel(z, ids, near, far, pay, table, halo, lent):
    b = ids[0]
    for q in range(z.nb):
        table[b ^ q] = (near if q % 2 == 0 else far)[q // 2]
    for a in range(z.nb):
        lend = hot(meta_row(z, pay, a)[:, z.scan : z.scan + z.hs], z.slots)
        lent[a] = nn(table[a], lend).astype(BF)
    for a in range(z.nb):
        halo[a] = halo_of(z, lent, a)


def weight_sum(z, out, stacks, gall):
    factor = float(z.nb * z.slots) ** (-0.5)
    pieces = 3 if z.koff % 3 == 0 else z.koff
    size = z.depth // pieces
    for i in range(pieces):
        rows = slice(i * size, (i + 1) * size)
        total = None
        for n, stack in enumerate(stacks):
            for j in range(stack.shape[0]):
                part = nt(stack[j, rows, :], gall[n * stack.shape[0] + j])
                total = part if total is None else total + part
        out[rows, :] = (total * factor).astype(BF)


def weight_kernel(z, ids, gall, *rest):
    weight_sum(z, rest[-1], rest[:-1], gall)


def last_kernel(z, ids, near, far, weight, pay, scan, *rest):
    stacks, (out, wout, gall, pushed, kmo) = rest[:-5], rest[-5:]
    b = ids[0]
    collect(z, gall, ids, near, far)
    row = read_table(z, pay, b)[z.koff : z.koff + 1, 0 : z.scan]
    mine = jnp.transpose(jnp.broadcast_to(row, (8, z.scan)))[:, 0:1]
    square = (z.scan, z.scan)
    lane = lanes_of(square)
    sub = lax.broadcasted_iota(jnp.int32, square, 0)
    earlier = (mine == row) & (lane < sub)
    ordinal = jnp.sum(jnp.where(earlier, 1.0, 0.0), axis=1, keepdims=True)
    slot = ordinal + (b * z.cap).astype(F32)
    at = lax.broadcasted_iota(jnp.int32, (z.hs, z.slots), 0)
    wanted = jnp.where(at < z.rim, z.rim + b * z.cap + at, -5)
    if z.cap < z.rim:
        wanted = jnp.where(at < z.cap, wanted, -5)
    wanted = jnp.where((at >= z.rim) & (at < 2 * z.rim), at - z.rim, wanted)
    wanted = jnp.where((at >= 2 * z.rim) & (at < 3 * z.rim), at + z.slots - z.rim, wanted)
    target = lanes_of((1, z.hs))

    def brick(a, result):
        push(z, pushed, weight, gall[a])
        kmo[...] = map_values(z, pay, a)

        def step(k, got):
            rows = pl.ds(k * z.ch, z.ch)
            chosen = jnp.where(wanted == kmo[pl.ds(k, 1), :], 1.0, 0.0).astype(BF)
            return got + nt(pushed[rows, :], chosen)

        got = loop(z.koff, step, jnp.zeros((z.ch, z.hs), F32))
        before, after = jnp.maximum(a - 1, 0), jnp.minimum(a + 1, z.nb - 1)
        low = meta_row(z, pay, before)[:, z.scan : z.scan + z.hs]
        high = meta_row(z, pay, after)[:, z.scan : z.scan + z.hs]
        holder = jnp.where(target < z.rim, a, jnp.where(target < 2 * z.rim, a - 1, a + 1))
        where = jnp.where(target < z.rim, b * z.cap + target, jnp.where(target < 2 * z.rim, low, high))
        place = jnp.where((mine == holder.astype(F32)) & (slot == where.astype(F32)), 1.0, 0.0).astype(BF)
        big = got.astype(BF)
        result = result + nt(big, place) + nt((got - big.astype(F32)).astype(BF), place)
        target_own = lanes_of((1, z.cap))
        place = jnp.where((mine == jnp.asarray(a, F32)) & (ordinal == target_own.astype(F32)), 1.0, 0.0).astype(BF)
        return result + nt(scan[a], place)

    result = lax.fori_loop(0, z.nb, brick, jnp.zeros((z.ch, z.scan), F32))
    out[...] = result.astype(BF)
    weight_sum(z, wout, stacks, gall)


def swap(value, axis, mask):
    count = lax.axis_size(axis)
    return lax.ppermute(value, axis, [(i ^ mask, i) for i in range(count)])


def swap_both(value, brick_mask, ch_mask):
    if ch_mask == 0:
        return swap(value, "brick", brick_mask)
    if brick_mask == 0:
        return swap(value, "ch", ch_mask)
    nb, nc = lax.axis_size("brick"), lax.axis_size("ch")
    pairs = [
        ((b ^ brick_mask) * nc + (c ^ ch_mask), b * nc + c) for b in range(nb) for c in range(nc)
    ]
    return lax.ppermute(value, ("brick", "ch"), pairs)


def over_even(blocks, count):
    return jnp.stack(
        [blocks[0]] + [swap(blocks[i], "brick", 2 * i) for i in range(1, count // 2)]
    )


def over_bricks(block, nb):
    near = over_even([block] * (nb // 2), nb)
    return near, swap(near, "brick", 1)


def over_all(blocks, nb, nc):
    plane = over_even(blocks, nb)
    parts = [plane]
    for i in range(nc // 2):
        for y in range(2):
            if i or y:
                parts.append(swap_both(plane, y, 2 * i))
    near = jnp.concatenate(parts, axis=0)
    return near, swap(near, "ch", 1)


def gathered_local(
    features,
    owner_map,
    kernel_map,
    send_lists,
    drop_first,
    drop_second,
    weight_first,
    weight_second,
    cotangent,
):
    nb, nc = lax.axis_size("brick"), lax.axis_size("ch")
    z = Sizes(features, kernel_map, send_lists, nb, nc)
    ids = jnp.stack([lax.axis_index("brick"), lax.axis_index("ch")]).astype(jnp.int32)
    sds = jax.ShapeDtypeStruct
    vm = pltpu.VMEM
    flat_first = weight_first.reshape(z.depth, z.all)
    flat_second = weight_second.reshape(z.depth, z.all)
    turned_first = flat_first.T
    turned_second = flat_second.T

    payload = call(
        functools.partial(pack_kernel, z),
        sds((z.rows, z.slots), BF),
        [vm((z.kr, z.slots), jnp.int32)],
        [features, owner_map.reshape(1, z.scan), kernel_map, send_lists, drop_first],
        ids,
        name="pack",
    )
    near, far = over_bricks(payload, nb)
    wide = z.slots + z.hs
    ints = [vm((z.kr, z.slots), jnp.int32)] * 2
    *parts, keep, pay, vox, halo = call(
        functools.partial(first_kernel, z),
        [sds((z.ch, wide), F32)]
        + [sds((z.ch, wide), BF)] * (nc - 1)
        + [
            sds((z.ch, wide), F32),
            sds((nb, z.rows, z.slots), BF),
            sds((nb, z.ch + 16, z.slots), BF),
            sds((nb, z.ch + 16, z.hs), BF),
        ],
        [
            vm((nb, z.scan), F32),
            vm((nb, z.ch + 16, z.hs), BF),
            vm((z.depth, wide), BF),
            *ints,
            vm((z.kr, z.hs), jnp.int32),
            vm((z.kr, z.hs), jnp.int32),
        ],
        [near, far, drop_first, turned_first],
        ids,
        name="first",
    )
    arrived = [parts[0]] + [swap(parts[j], "ch", j) for j in range(1, nc)]
    small = [vm((z.koff, z.slots), jnp.int32)] * 2
    *parts, conv, hidden = call(
        functools.partial(second_kernel, z),
        [sds((z.ch, z.slots), F32)]
        + [sds((z.ch, z.slots), BF)] * (nc - 1)
        + [sds((z.ch, z.slots), F32), sds((z.ch, z.slots), BF)],
        [vm((z.depth, z.slots), BF), *small],
        [*arrived, keep, kernel_map, turned_second],
        ids,
        name="second",
    )
    arrived = [parts[0]] + [swap(parts[j], "ch", j) for j in range(1, nc)]
    block_out, *sends = call(
        functools.partial(third_kernel, z),
        [sds((z.ch, z.slots), BF)] + [sds((z.ch, z.slots + 2 * z.cap), BF)] * (nb // 2),
        [],
        [*arrived, vox, drop_second, cotangent],
        ids,
        name="third",
    )
    group = 2

    def gathered(table, halo, name):
        return [
            call(
                functools.partial(gather_kernel, z, i, group),
                sds((group, z.depth, z.slots), BF),
                ints,
                [pay, table, halo],
                ids,
                flops=2 * 10**9,
                name=name,
            )
            for i in range(0, nb, group)
        ]

    stacks_first = gathered(vox, halo, "gather_first")
    hidden_near, hidden_far = over_bricks(hidden, nb)
    hidden_all, hidden_halo = call(
        functools.partial(table_kernel, z),
        [sds((nb, z.ch, z.slots), BF), sds((nb, z.ch, z.hs), BF)],
        [vm((nb, z.ch, z.hs), BF)],
        [hidden_near, hidden_far, pay],
        ids,
        name="table",
    )
    stacks_second = gathered(hidden_all, hidden_halo, "gather_second")
    near, far = over_all(sends, nb, nc)
    grad_first, gall, scan = call(
        functools.partial(fourth_kernel, z),
        [
            sds((z.ch, z.slots), BF),
            sds((nb, z.all, z.slots), BF),
            sds((nb, z.ch, z.cap), BF),
        ],
        [vm((3, z.depth, z.slots), BF)] + [vm((z.kr, z.slots), jnp.int32)] * 3,
        [near, far, flat_second, pay, conv, keep],
        ids,
        name="fourth",
    )
    weight_grad_second = call(
        functools.partial(weight_kernel, z),
        sds((z.depth, z.all), BF),
        [],
        [gall, *stacks_second],
        ids,
        flops=3 * 10**9,
        name="second_weight",
    )
    near, far = over_all([grad_first] * (nb // 2), nb, nc)
    grad_features, weight_grad_first = call(
        functools.partial(last_kernel, z),
        [sds((z.ch, z.scan), BF), sds((z.depth, z.all), BF)],
        [
            vm((nb, z.all, z.slots), BF),
            vm((z.depth, z.slots), BF),
            vm((z.kr, z.slots), jnp.int32),
        ],
        [near, far, flat_first, pay, scan, *stacks_first],
        ids,
        name="last",
    )
    return (
        block_out,
        grad_features,
        weight_grad_first.reshape(weight_first.shape),
        weight_grad_second.reshape(weight_second.shape),
    )


def with_halo(block, sides, width):
    for axis, dim in sides:
        count = lax.axis_size(axis)
        forward = [(i, i + 1) for i in range(count - 1)]
        backward = [(target, source) for source, target in forward]
        low = lax.ppermute(
            lax.slice_in_dim(block, block.shape[dim] - width, None, axis=dim), axis, forward
        )
        high = lax.ppermute(lax.slice_in_dim(block, 0, width, axis=dim), axis, backward)
        block = jnp.concatenate([low, block, high], axis=dim)
    return block


def spread(field, send_lists):
    rim_width = send_lists.shape[1]
    outgoing = jnp.concatenate(
        [jnp.take(field, send_lists[0], axis=1), jnp.take(field, send_lists[1], axis=1)], axis=1
    )
    padded = with_halo(outgoing, (("brick", 1),), rim_width)
    return jnp.concatenate([padded[:, :rim_width], field, padded[:, 3 * rim_width :]], axis=1)


def convolve(extended, kernel_map, weight):
    gathered = jnp.take(extended, kernel_map, axis=1, mode="fill", fill_value=0)
    return (
        lax.psum_scatter(
            jnp.einsum("ckr,kco->or", gathered, weight, preferred_element_type=jnp.float32),
            "ch",
            scatter_dimension=0,
            tiled=True,
        ),
        gathered,
    )


def adjoint(gathered, kernel_map, grad_local, weight, extent):
    gathered_grad = lax.all_gather(grad_local, "ch", axis=0, tiled=True)
    weight_grad = jnp.einsum(
        "ckr,or->kco", gathered, gathered_grad, preferred_element_type=jnp.float32
    )
    pushed = jnp.einsum("kco,or->ckr", weight, gathered_grad, preferred_element_type=jnp.float32)
    returned = (
        jnp.zeros((pushed.shape[0], extent), jnp.float32).at[:, kernel_map].add(pushed, mode="drop")
    )
    return (weight_grad, returned)


def fold_back(returned, send_lists, slot_count):
    rim_width = send_lists.shape[1]
    borders = jnp.concatenate(
        [returned[:, :rim_width], returned[:, rim_width + slot_count :]], axis=1
    )
    padded = with_halo(borders, (("brick", 1),), rim_width)
    interior = returned[:, rim_width : rim_width + slot_count]
    interior = interior.at[:, send_lists[0]].add(padded[:, :rim_width])
    return interior.at[:, send_lists[1]].add(padded[:, 3 * rim_width :])


def summed_local(
    features,
    owner_map,
    kernel_map,
    send_lists,
    drop_first,
    drop_second,
    weight_first,
    weight_second,
    cotangent,
):
    bricks = lax.axis_size("brick")
    channels = features.shape[0]
    slot_count = 2 * features.shape[1]
    capacity = slot_count // bricks
    targets = owner_map[:, 0]
    matches = (targets[:, None] == jnp.arange(bricks, dtype=jnp.int32)[None, :]).astype(jnp.int32)
    running = jnp.cumsum(matches, axis=0)
    ordinal = jnp.sum((running - 1) * matches, axis=1)
    columns = targets * capacity + ordinal
    outgoing = jnp.zeros((channels, slot_count), features.dtype).at[:, columns].set(features)
    tallies = jnp.sum(matches, axis=0)[None, :].astype(jnp.bfloat16)
    arrived, arrived_tallies = (
        lax.all_to_all(
            outgoing.reshape(channels, bricks, capacity),
            "brick",
            split_axis=1,
            concat_axis=1,
            tiled=True,
        ),
        lax.all_to_all(tallies, "brick", split_axis=1, concat_axis=1, tiled=True),
    )
    voxels = arrived.reshape(channels, slot_count)
    occupied = (
        jnp.arange(capacity, dtype=jnp.int32)[None, :]
        < arrived_tallies[0].astype(jnp.int32)[:, None]
    )
    occupied = occupied.reshape(slot_count).astype(jnp.float32)
    keep_first = occupied[None, :] * drop_first.astype(jnp.float32) / KEEP_RATE
    keep_second = occupied[None, :] * drop_second.astype(jnp.float32) / KEEP_RATE
    extended_voxels = spread(voxels, send_lists)
    extent = extended_voxels.shape[1]
    conv_first, gathered_voxels = convolve(extended_voxels, kernel_map, weight_first)
    hidden = (jax.nn.silu(conv_first) * keep_first).astype(jnp.bfloat16)
    extended_hidden = spread(hidden, send_lists)
    conv_second, gathered_hidden = convolve(extended_hidden, kernel_map, weight_second)
    summed = voxels.astype(jnp.float32) + keep_second * conv_second
    block_out = jax.nn.silu(summed).astype(jnp.bfloat16)
    grad_pre = cotangent.astype(jnp.float32) * slope_silu(summed)
    grad_second = (grad_pre * keep_second).astype(jnp.bfloat16)
    weight_grad_second, returned_second = adjoint(
        gathered_hidden, kernel_map, grad_second, weight_second, extent
    )
    grad_hidden = fold_back(returned_second, send_lists, slot_count)
    grad_first = (grad_hidden * keep_first * slope_silu(conv_first)).astype(jnp.bfloat16)
    weight_grad_first, returned_first = adjoint(
        gathered_voxels, kernel_map, grad_first, weight_first, extent
    )
    weight_grad_first, weight_grad_second = lax.psum(
        (weight_grad_first, weight_grad_second), "brick"
    )
    grad_voxels = (grad_pre + fold_back(returned_first, send_lists, slot_count)).astype(
        jnp.bfloat16
    )
    homeward = lax.all_to_all(
        grad_voxels.reshape(channels, bricks, capacity),
        "brick",
        split_axis=1,
        concat_axis=1,
        tiled=True,
    )
    grad_features = jnp.take(homeward.reshape(channels, slot_count), columns, axis=1)
    factor = float(bricks * slot_count) ** (-0.5)
    return (
        block_out,
        grad_features,
        (weight_grad_first * factor).astype(jnp.bfloat16),
        (weight_grad_second * factor).astype(jnp.bfloat16),
    )


def local(features, owner_map, kernel_map, *rest):
    nb, nc = lax.axis_size("brick"), lax.axis_size("ch")
    channels = features.shape[0]
    gather = nb * kernel_map.shape[1] <= 2 * kernel_map.shape[0] * channels
    even = all(n > 1 and n & (n - 1) == 0 for n in (nb, nc))
    scan, slots, rim = features.shape[1], kernel_map.shape[1], rest[0].shape[1]
    fits = slots <= nb * rim and slots == 2 * scan and 4 * rim <= scan
    plan = gathered_local if gather and even and fits else summed_local
    return plan(features, owner_map, kernel_map, *rest)


def solution(mesh):
    return jax.shard_map(
        local,
        mesh=mesh,
        in_specs=(
            P("ch", "brick"),
            P("brick", None),
            P(None, "brick"),
            P(None, "brick"),
            P("ch", "brick"),
            P("ch", "brick"),
            P(None, "ch", None),
            P(None, "ch", None),
            P("ch", "brick"),
        ),
        out_specs=(P("ch", "brick"), P("ch", "brick"), P(None, "ch", None), P(None, "ch", None)),
        check_vma=False,
    )
```
